512 devices in a mesh: frame: 512 (over y, z, x, core).
Axes of the slice: x: 4, y: 8, z: 8, core: 2. Of those that a mesh axis runs over, the one named last changes fastest.
Arguments:
- tokens: bfloat16 [786432, 128], P('frame'), may hold values from -8 to 8
- fine_map: bfloat16 [24576, 128, 128], P('frame'), may hold values from -8 to 8
- matches: int32 [512, 2, 2, 512], P('frame'), may hold values from 0 to 1535
- subcells: int32 [512, 2, 2, 512], P('frame'), may hold values from 0 to 3
- counts: int32 [512, 2], P('frame'), may hold values from 64 to 512, as said below
Outputs:
- confidence: float32 [512, 2, 512], P('frame')
- offsets: float32 [512, 2, 2, 512], P('frame')
The draws below stay inside these ranges and needn't reach their ends.
Inputs may be any that keep to these rules, and one draw needn't show every extreme that they name: `counts`: for each round some frame has exactly 512 valid slots; slots at or beyond the count are ignored.
All inputs are finite; a program needn't handle non-finite values.
Results may differ from the reference program's by a relative error of at most 0.0003.
Values may be sent and summed in bfloat16 or wider, within the bound.
A program may use at most 64 MiB of HBM per device.

```python
import math
import jax
import jax.numpy as jnp
import numpy as np
from jax import lax

C = 128
CF = 128
WC = 64
M = 512
ROUNDS = 2
TOK = 1536
FH = 48
FW = 128
FRAMES = 512


def draw_tokens(key, part):
    key_base = jax.random.fold_in(jax.random.fold_in(key, 11), 0)
    rows = FRAMES * TOK
    values = jnp.clip(jax.random.normal(key_base, (rows, C), jnp.float32), -4.0, 4.0)
    return values.astype(jnp.bfloat16)


def draw_fine_map(key, part):
    key_base = jax.random.fold_in(jax.random.fold_in(key, 23), 0)
    rows = FRAMES * FH
    values = jnp.clip(jax.random.normal(key_base, (rows, FW, CF), jnp.float32), -4.0, 4.0)
    return values.astype(jnp.bfloat16)


def draw_counts(key, part):
    key_low, key_high, key_pick, key_full = jax.random.split(jax.random.fold_in(key, 37), 4)
    base = jax.random.randint(key_low, (FRAMES, ROUNDS), M // 8, M // 2 + 1)
    heavy = jax.random.randint(key_high, (FRAMES, ROUNDS), M // 2, M + 1)
    picked = jax.random.randint(key_pick, (FRAMES, ROUNDS), 0, 8) == 0
    amount = jnp.where(picked, heavy, base)
    fullest = jax.random.randint(key_full, (ROUNDS,), 0, FRAMES)
    amount = jnp.where(jnp.arange(FRAMES, dtype=jnp.int32)[:, None] == fullest[None, :], M, amount)
    return amount.astype(jnp.int32)


def touch_ends(drawn, own_key, low, top_value):
    place = [jax.random.randint(jax.random.fold_in(own_key, axis), (), 0, length) for axis, length in enumerate(drawn.shape)]
    main_axis = drawn.shape.index(max(drawn.shape))
    beside = place[:main_axis] + [(place[main_axis] + 1) % drawn.shape[main_axis]] + place[main_axis + 1:]
    return drawn.at[tuple(place)].set(low).at[tuple(beside)].set(top_value)


def setup_inputs(seed: int = 0) -> dict:
    seeds = jax.random.split(jax.random.key(seed), 6)
    tokens = draw_tokens(jax.random.fold_in(seeds[5], 71), 0)
    fine_map = draw_fine_map(jax.random.fold_in(seeds[5], 71), 0)
    matches = touch_ends(jax.random.randint(seeds[2], (FRAMES, ROUNDS, 2, M), 0, TOK), jax.random.fold_in(seeds[2], 1), 0, TOK - 1).astype(jnp.int32)
    subcells = touch_ends(jax.random.randint(seeds[3], (FRAMES, ROUNDS, 2, M), 0, 4), jax.random.fold_in(seeds[3], 1), 0, 3).astype(jnp.int32)
    counts = draw_counts(jax.random.fold_in(seeds[5], 71), 0)
    return {"tokens": tokens, "fine_map": fine_map, "matches": matches, "subcells": subcells, "counts": counts}


def crop_tiles(flat_map, cells, subs):
    cell_y = 2 * (cells // WC) + subs // 2
    cell_x = 2 * (cells % WC) + subs % 2
    spots = jnp.arange(25, dtype=jnp.int32)
    delta_y = spots // 5 - 2
    delta_x = spots % 5 - 2
    near_y = cell_y[:, None] + delta_y[None, :]
    near_x = cell_x[:, None] + delta_x[None, :]
    inside = (near_y >= 0) & (near_y < FH) & (near_x >= 0) & (near_x < FW)
    index = jnp.clip(near_y, 0, FH - 1) * FW + jnp.clip(near_x, 0, FW - 1)
    return flat_map[index] * inside[:, :, None].astype(flat_map.dtype)


def fine_offsets(tiles, query):
    heat = jnp.einsum("mjc,mc->mj", tiles.astype(jnp.float32), query.astype(jnp.float32)) * (CF ** -0.5)
    heat = heat - jnp.max(heat, axis=1, keepdims=True)
    expo = jnp.exp(heat)
    weight = expo / jnp.sum(expo, axis=1, keepdims=True)
    spots = jnp.arange(25, dtype=jnp.int32)
    delta_y = (spots // 5 - 2).astype(jnp.float32)
    delta_x = (spots % 5 - 2).astype(jnp.float32)
    return jnp.stack([jnp.sum(weight * delta_x[None, :], axis=1), jnp.sum(weight * delta_y[None, :], axis=1)])


def reference(tokens, fine_map, matches, subcells, counts):
    scale = 10.0 / C
    frame_tok = tokens.reshape(FRAMES, TOK, C)
    maps = fine_map.reshape(FRAMES, FH * FW, CF)
    conf_rounds = []
    offset_rounds = []
    for rnd in range(ROUNDS):
        bit = FRAMES >> (rnd + 1)
        ids = np.arange(FRAMES)
        lows = ids[(ids & bit) == 0]

        def pair_stats(low):
            scores = jnp.dot(frame_tok[low], frame_tok[low + bit].T, preferred_element_type=jnp.float32) * scale
            return jax.nn.logsumexp(scores, axis=1), jax.nn.logsumexp(scores, axis=0)

        row_lse, col_lse = lax.map(pair_stats, jnp.asarray(lows, dtype=jnp.int32))
        lse = jnp.zeros((FRAMES, TOK), jnp.float32).at[lows].set(row_lse).at[lows + bit].set(col_lse)

        def frame_out(frame):
            other = jnp.bitwise_xor(frame, jnp.int32(bit)).astype(jnp.int32)
            own_cells = matches[frame, rnd, 0]
            far_cells = matches[frame, rnd, 1]
            own_rows = frame_tok[frame][own_cells].astype(jnp.float32)
            far_rows = frame_tok[other][far_cells].astype(jnp.float32)
            score = jnp.sum(own_rows * far_rows, axis=1) * scale
            conf = 2.0 * score - lse[frame][own_cells] - lse[other][far_cells] + 2.0 * math.log(TOK)
            valid = jnp.arange(M, dtype=jnp.int32) < counts[frame, rnd]
            own_sub = subcells[frame, rnd, 0]
            cell_y = 2 * (own_cells // WC) + own_sub // 2
            cell_x = 2 * (own_cells % WC) + own_sub % 2
            query = maps[frame][cell_y * FW + cell_x]
            tiles = crop_tiles(maps[other], far_cells, subcells[frame, rnd, 1])
            offs = fine_offsets(tiles, query)
            return jnp.where(valid, conf, 0.0), jnp.where(valid[None, :], offs, 0.0)

        conf, offs = lax.map(frame_out, jnp.arange(FRAMES, dtype=jnp.int32))
        conf_rounds.append(conf)
        offset_rounds.append(offs)
    return jnp.stack(conf_rounds, axis=1), jnp.stack(offset_rounds, axis=1)
```

```python
import math

import jax
import jax.numpy as jnp
from jax import lax
from jax.experimental import pallas as pl
from jax.experimental.pallas import tpu as pltpu
from jax.sharding import PartitionSpec as P

MESH = pl.DeviceIdType.MESH
F32 = jnp.float32
BF16 = jnp.bfloat16
NEG = -1e30
YRING = 8


def kernel(
    devices, tok_hbm, map_hbm, mat_hbm, sub_hbm, cnt_ref, conf_ref, off_ref,
    mapb, mapf, left, right, mleft, mright, mat, sub, pvec, psm, req_out, req_in, qf, q_out, q_in,
    heat, acc, scores, onehot, got_left, got_right, lse_left, lse_right,
    off_out, off_in, conf_out, conf_in, lsem, ssem, rsem,
):
    tok_count, width = tok_hbm.shape
    points = map_hbm.shape[0]
    fine_w = 128
    fine_h = points // fine_w
    slots = mat.shape[2]
    scale = 10.0 / width
    stride = devices // YRING
    me = lax.axis_index("frame")
    row = me // stride
    rest = me % stride
    core = rest % 2
    low = (row // 2) % 2
    home = (row // 4 + low + core + 1) % 2
    near = row + 2 - 4 * low
    opposite = (row + 4) % YRING
    far = (near + 4) % YRING

    def at(yy, cc):
        return (yy * stride + (rest - core) + cc,)

    sibling = at(row, 1 - core)
    near_same, near_other = at(near, core), at(near, 1 - core)
    opp_same, far_other = at(opposite, core), at(far, 1 - core)

    def remote(src, dst, i, dev):
        return pltpu.make_async_remote_copy(
            src_ref=src, dst_ref=dst, send_sem=ssem.at[i], recv_sem=rsem.at[i], device_id=dev, device_id_type=MESH
        )

    map_cp = pltpu.make_async_copy(map_hbm, mapb, lsem.at[0])
    mat_cp = pltpu.make_async_copy(mat_hbm, mat, lsem.at[1])
    sub_cp = pltpu.make_async_copy(sub_hbm, sub, lsem.at[2])
    own_cp = pltpu.make_async_copy(tok_hbm, left, lsem.at[3])
    mat_cp.start()
    sub_cp.start()
    map_cp.start()

    bar = pltpu.get_barrier_semaphore()
    peers = (sibling, near_same, near_other, opp_same, far_other)
    for peer in peers:
        pl.semaphore_signal(bar, inc=1, device_id=peer, device_id_type=MESH)
    pl.semaphore_wait(bar, len(peers))

    tok_a = remote(tok_hbm, left, 0, far_other)
    mat_a = remote(mat_hbm, mleft, 1, far_other)
    tok_b = remote(tok_hbm, right, 2, near_same)
    mat_b = remote(mat_hbm, mright, 3, near_same)
    tok_f = remote(right, right, 2, sibling)
    mat_f = remote(mright, mright, 3, sibling)

    @pl.when(home == 1)
    def _():
        mat_a.start()
        tok_a.start()
        own_cp.start()

    @pl.when(home == 0)
    def _():
        mat_b.start()
        tok_b.start()

    mat_cp.wait()
    sub_cp.wait()
    for rnd in range(2):
        cells, subs = mat[rnd], sub[rnd]
        yy = 2 * (cells >> 6) + (subs >> 1)
        xx = 2 * (cells & 63) + (subs & 1)
        pvec[rnd : rnd + 1, :] = (yy * fine_w + xx)[0:1, :]
        req_out[rnd, 0:1, :] = yy[1:2, :]
        req_out[rnd, 1:2, :] = xx[1:2, :]
    p_cp = pltpu.make_async_copy(pvec, psm, lsem.at[1])
    p_cp.start()
    map_cp.wait()

    @pl.loop(0, points // 256)
    def _(i):
        blk = pl.ds(pl.multiple_of(i * 256, 256), 256)
        mapf[blk, :] = mapb[blk, :].astype(F32)

    p_cp.wait()
    q_cps = []
    for rnd in range(2):

        @pl.loop(0, slots // 8)
        def _(g):
            for s in range(8):
                j = g * 8 + s
                qf[pl.ds(j, 1), :] = mapf[pl.ds(psm[rnd, j], 1), :]

        q_out[rnd] = qf[...].astype(BF16)
        dev = opp_same if rnd == 0 else near_same
        for cp in (remote(req_out.at[rnd], req_in.at[rnd], 4 + rnd, dev), remote(q_out.at[rnd], q_in.at[rnd], 6 + rnd, dev)):
            cp.start()
            q_cps.append(cp)

    @pl.when(home == 1)
    def _():
        mat_b.wait_recv()
        tok_b.wait_recv()
        mat_f.start()
        tok_f.start()
        own_cp.wait()
        mleft[...] = mat[...]

    @pl.when(home == 0)
    def _():
        mat_a.wait_recv()
        tok_a.wait_recv()
        mat_f.wait_recv()
        tok_f.wait_recv()

    def col_lse(rows, cols, out):
        for jb in range(tok_count // 512):

            def dots(i, m8):
                blk = pl.ds(pl.multiple_of(i * 256, 256), 256)
                s = lax.dot_general(
                    rows[blk, :], cols[jb * 512 : (jb + 1) * 512, :], (((1,), (1,)), ((), ())), preferred_element_type=F32
                )
                scores[blk, :] = s
                return jnp.maximum(m8, jnp.max(s.reshape(32, 8, 512), axis=0))

            m8 = lax.fori_loop(0, tok_count // 256, dots, jnp.full((8, 512), NEG, F32))
            top = jnp.max(m8, axis=0, keepdims=True)

            def sums(i, s8):
                s = scores[pl.ds(pl.multiple_of(i * 64, 64), 64), :]
                return s8 + jnp.sum(jnp.exp((s - top) * scale).reshape(8, 8, 512), axis=0)

            s8 = lax.fori_loop(0, tok_count // 64, sums, jnp.zeros((8, 512), F32))
            out[0:1, jb * 512 : (jb + 1) * 512] = top * scale + jnp.log(jnp.sum(s8, axis=0, keepdims=True))

    col_lse(right, left, lse_left)
    col_lse(left, right, lse_right)

    def gather(toks, lse, index, got):
        @pl.loop(0, tok_count // 64)
        def _(i):
            blk = pl.ds(pl.multiple_of(i * 64, 64), 64)
            tt = lax.broadcasted_iota(jnp.int32, (64, 2 * slots), 0) + i * 64
            onehot[blk, :] = jnp.where(tt == index, 1.0, 0.0).astype(BF16)

        v = lse[0:1, :]
        hi = v.astype(BF16)
        mid = (v - hi.astype(F32)).astype(BF16)
        lo = (v - hi.astype(F32) - mid.astype(F32)).astype(BF16)
        pieces = jnp.concatenate([hi.astype(F32), mid.astype(F32), lo.astype(F32), jnp.zeros((13, tok_count), F32)], axis=0)
        got[0:width, :] = lax.dot_general(toks[...], onehot[...], (((0,), (0,)), ((), ())), preferred_element_type=F32)
        got[width : width + 16, :] = jnp.dot(pieces.astype(BF16), onehot[...], preferred_element_type=F32)

    ml, mr = mleft[1 * home], mright[1 * home]
    gather(left, lse_left, jnp.concatenate([ml[0:1, :], mr[1:2, :]], axis=1), got_left)
    gather(right, lse_right, jnp.concatenate([ml[1:2, :], mr[0:1, :]], axis=1), got_right)
    pair = jnp.sum(got_left[0:width, :] * got_right[0:width, :], axis=0, keepdims=True) * scale
    lses = jnp.sum(got_left[width : width + 8, :] + got_right[width : width + 8, :], axis=0, keepdims=True)
    conf = 2.0 * pair - lses + 2.0 * math.log(tok_count)
    conf_out[0] = conf[:, 0:slots]
    conf_out[1] = conf[:, slots:]
    conf_r = remote(conf_out.at[1], conf_in.at[home], 9 - home, at(near, home * core + (1 - home) * (1 - core)))
    conf_l = remote(conf_out.at[0], conf_in.at[0], 10, far_other)
    conf_w0 = remote(conf_out.at[1], conf_in.at[0], 9, near_other)
    conf_w1 = remote(conf_out.at[1], conf_in.at[1], 8, near_same)
    conf_r.start()

    @pl.when(home == 0)
    def _():
        conf_l.start()

    def refine(rnd):
        def dots(i, carry):
            blk = pl.ds(pl.multiple_of(i * 512, 512), 512)
            heat[blk, :] = lax.dot_general(
                mapb[blk, :], q_in[rnd], (((1,), (1,)), ((), ())), preferred_element_type=F32
            )
            return carry

        lax.fori_loop(0, points // 512, dots, 0)

        @pl.loop(0, slots // 128)
        def _(jt):
            lane = pl.ds(pl.multiple_of(jt * 128, 128), 128)
            ylow = jnp.broadcast_to(req_in[rnd, 0:1, lane] - 2, (8, 128))
            xmid = jnp.broadcast_to(req_in[rnd, 1:2, lane], (8, 128))

            @pl.loop(0, 4)
            def _(xb):
                accs = [[jnp.zeros((8, 128), F32) for _ in range(4)] for _ in range(5)]
                for yy in range(fine_h):
                    d = yy - ylow
                    hit = (d >= 0) & (d < 5)
                    for k in range(4):
                        h = heat[pl.ds(pl.multiple_of(yy * fine_w + xb * 32 + k * 8, 8), 8), lane]
                        accs[yy % 5][k] = jnp.where(hit, h, accs[yy % 5][k])
                for r in range(5):
                    for k in range(4):
                        acc[r, pl.ds(pl.multiple_of(xb * 32 + k * 8, 8), 8), lane] = accs[r][k] * (width ** -0.5)

            iota = lax.broadcasted_iota(jnp.int32, (8, 128), 0)
            m8 = jnp.full((8, 128), NEG, F32)
            for xt in range(fine_w // 8):
                dx = iota + xt * 8 - xmid
                inside = (dx >= -2) & (dx <= 2)
                v = acc[0, xt * 8 : xt * 8 + 8, lane]
                for r in range(1, 5):
                    v = jnp.maximum(v, acc[r, xt * 8 : xt * 8 + 8, lane])
                m8 = jnp.maximum(m8, jnp.where(inside, v, NEG))
            x1 = xmid[0:1, :]
            missing = jnp.maximum(2 - x1, 0) + jnp.maximum(x1 - (fine_w - 3), 0)
            top = jnp.max(m8, axis=0, keepdims=True)
            top = jnp.where(missing > 0, jnp.maximum(top, 0.0), top)
            topb = jnp.broadcast_to(top, (8, 128))
            z = [jnp.zeros((8, 128), F32) for _ in range(5)]
            sx = jnp.zeros((8, 128), F32)
            for xt in range(fine_w // 8):
                dx = iota + xt * 8 - xmid
                inside = (dx >= -2) & (dx <= 2)
                tot = jnp.zeros((8, 128), F32)
                for r in range(5):
                    e = jnp.where(inside, jnp.exp(acc[r, xt * 8 : xt * 8 + 8, lane] - topb), 0.0)
                    z[r] = z[r] + e
                    tot = tot + e
                sx = sx + tot * dx.astype(F32)
            sy = jnp.zeros((8, 128), F32)
            tot = jnp.zeros((8, 128), F32)
            for r in range(5):
                t = r - ylow + 50
                dy = t - 5 * ((t * 205) >> 10) - 2
                sy = sy + z[r] * dy.astype(F32)
                tot = tot + z[r]
            tot1 = jnp.sum(tot, axis=0, keepdims=True)
            sx1 = jnp.sum(sx, axis=0, keepdims=True)
            sy1 = jnp.sum(sy, axis=0, keepdims=True)
            zero = jnp.where(missing > 0, jnp.exp(-jnp.maximum(top, 0.0)), 0.0) * 5.0
            gone = jnp.where(x1 == 0, -3.0, 0.0) + jnp.where(x1 == 1, -2.0, 0.0)
            gone = gone + jnp.where(x1 == fine_w - 1, 3.0, 0.0) + jnp.where(x1 == fine_w - 2, 2.0, 0.0)
            tot1 = tot1 + zero * missing.astype(F32)
            sx1 = sx1 + zero * gone
            off_out[rnd, 0:1, lane] = sx1 / tot1
            off_out[rnd, 1:2, lane] = sy1 / tot1

    off_cps = []
    for rnd in range(2):
        q_cps[2 * rnd].wait_recv()
        q_cps[2 * rnd + 1].wait_recv()
        refine(rnd)
        cp = remote(off_out.at[rnd], off_in.at[rnd], 11 + rnd, opp_same if rnd == 0 else near_same)
        cp.start()
        off_cps.append(cp)

    for rnd in range(2):
        off_cps[rnd].wait_recv()
        valid = lax.broadcasted_iota(jnp.int32, (2, slots), 1) < cnt_ref[0, rnd]
        off_ref[rnd] = jnp.where(valid, off_in[rnd], 0.0)

    @pl.when(home == 1)
    def _():
        conf_l.wait_recv()
        conf_in[1] = conf_out[0]

    @pl.when(home == 0)
    def _():
        conf_w0.wait_recv()
        conf_w1.wait_recv()

    for rnd in range(2):
        valid = lax.broadcasted_iota(jnp.int32, (1, slots), 1) < cnt_ref[0, rnd]
        conf_ref[rnd : rnd + 1, :] = jnp.where(valid, conf_in[rnd], 0.0)

    for cp in q_cps + off_cps + [conf_r]:
        cp.wait_send()

    @pl.when(home == 1)
    def _():
        mat_a.wait_send()
        tok_a.wait_send()
        mat_f.wait_send()
        tok_f.wait_send()

    @pl.when(home == 0)
    def _():
        mat_b.wait_send()
        tok_b.wait_send()
        conf_l.wait_send()


def solution(mesh):
    devices = mesh.size

    def body(tokens, fine_map, matches, subcells, counts):
        tok_count, width = tokens.shape
        fine_h, fine_w, _ = fine_map.shape
        points = fine_h * fine_w
        slots = matches.shape[3]
        any_spec = pl.BlockSpec(memory_space=pl.ANY)
        vmem = pltpu.VMEM
        conf, offs = pl.pallas_call(
            lambda *refs: kernel(devices, *refs),
            name="match_refine",
            out_shape=(
                jax.ShapeDtypeStruct((2, slots), F32),
                jax.ShapeDtypeStruct((2, 2, slots), F32),
            ),
            in_specs=[any_spec] * 4 + [pl.BlockSpec(memory_space=pltpu.SMEM)],
            out_specs=(pl.BlockSpec(memory_space=pltpu.VMEM), pl.BlockSpec(memory_space=pltpu.VMEM)),
            scratch_shapes=[
                vmem((points, width), BF16),
                vmem((points, width), F32),
                vmem((tok_count, width), BF16),
                vmem((tok_count, width), BF16),
                vmem((2, 2, slots), jnp.int32),
                vmem((2, 2, slots), jnp.int32),
                vmem((2, 2, slots), jnp.int32),
                vmem((2, 2, slots), jnp.int32),
                vmem((2, slots), jnp.int32),
                pltpu.SMEM((2, slots), jnp.int32),
                vmem((2, 2, slots), jnp.int32),
                vmem((2, 2, slots), jnp.int32),
                vmem((slots, width), F32),
                vmem((2, slots, width), BF16),
                vmem((2, slots, width), BF16),
                vmem((points, slots), F32),
                vmem((5, fine_w, slots), F32),
                vmem((tok_count, 512), F32),
                vmem((tok_count, 2 * slots), BF16),
                vmem((width + 16, 2 * slots), F32),
                vmem((width + 16, 2 * slots), F32),
                vmem((1, tok_count), F32),
                vmem((1, tok_count), F32),
                vmem((2, 2, slots), F32),
                vmem((2, 2, slots), F32),
                vmem((2, 1, slots), F32),
                vmem((2, 1, slots), F32),
                pltpu.SemaphoreType.DMA((4,)),
                pltpu.SemaphoreType.DMA((13,)),
                pltpu.SemaphoreType.DMA((13,)),
            ],
            compiler_params=pltpu.CompilerParams(
                collective_id=0, has_side_effects=True, vmem_limit_bytes=60 * 1024 * 1024
            ),
        )(tokens, fine_map.reshape(points, width), matches[0], subcells[0], counts)
        return conf[None], offs[None]

    return jax.shard_map(
        body,
        mesh=mesh,
        in_specs=(
            P("frame", None),
            P("frame", None, None),
            P("frame", None, None, None),
            P("frame", None, None, None),
            P("frame", None),
        ),
        out_specs=(P("frame", None, None), P("frame", None, None, None)),
        check_vma=False,
    )
```

```python
import math

import jax
import jax.numpy as jnp
from jax import lax
from jax.experimental import pallas as pl
from jax.experimental.pallas import tpu as pltpu
from jax.sharding import PartitionSpec as P

MESH = pl.DeviceIdType.MESH
F32 = jnp.float32
BF16 = jnp.bfloat16
NEG = -1e30
YRING = 8


def kernel(
    devices, tok_hbm, map_hbm, mat_hbm, sub_hbm, res_ref,
    mapb, mapf, left, right, mleft, mright, mat, sub, pvec, psm0, psm1, req_out, req_in, qf, q_out, q_in,
    acc, scores, lse_col, table_l, table_r, index, conf_both,
    off_out, off_in, conf_out, conf_in, lsem, ssem, rsem,
):
    tok_count, width = tok_hbm.shape
    fine_h, fine_w, _ = map_hbm.shape
    points = fine_h * fine_w
    slots = mat.shape[2]
    scale = 10.0 / width
    stride = devices // YRING
    me = lax.axis_index("frame")
    row = me // stride
    rest = me % stride
    core = rest % 2
    low = (row // 2) % 2
    home = (row // 4 + low + core + 1) % 2
    near = row + 2 - 4 * low
    opposite = (row + 4) % YRING
    far = (near + 4) % YRING

    def at(yy, cc):
        return (yy * stride + (rest - core) + cc,)

    sibling = at(row, 1 - core)
    near_same, near_other = at(near, core), at(near, 1 - core)
    opp_same, far_other = at(opposite, core), at(far, 1 - core)

    def remote(src, dst, i, dev):
        return pltpu.make_async_remote_copy(
            src_ref=src, dst_ref=dst, send_sem=ssem.at[i], recv_sem=rsem.at[i], device_id=dev, device_id_type=MESH
        )

    map_cp = pltpu.make_async_copy(map_hbm, mapb, lsem.at[0])
    mat_cp = pltpu.make_async_copy(mat_hbm, mat, lsem.at[1])
    sub_cp = pltpu.make_async_copy(sub_hbm, sub, lsem.at[2])
    own_cp = pltpu.make_async_copy(tok_hbm, left, lsem.at[3])
    mat_cp.start()
    sub_cp.start()
    map_cp.start()

    bar = pltpu.get_barrier_semaphore()
    peers = (sibling, near_same, near_other, opp_same, far_other)
    for peer in peers:
        pl.semaphore_signal(bar, inc=1, device_id=peer, device_id_type=MESH)
    pl.semaphore_wait(bar, len(peers))

    tok_a = remote(tok_hbm, left, 0, far_other)
    mat_a = remote(mat_hbm, mleft, 1, far_other)
    tok_b = remote(tok_hbm, right, 2, near_same)
    mat_b = remote(mat_hbm, mright, 3, near_same)
    tok_f = remote(right, right, 2, sibling)
    mat_f = remote(mright, mright, 3, sibling)

    @pl.when(home == 1)
    def _():
        mat_a.start()
        tok_a.start()
        own_cp.start()

    @pl.when(home == 0)
    def _():
        mat_b.start()
        tok_b.start()

    mat_cp.wait()
    sub_cp.wait()
    for rnd in range(2):
        cells, subs = mat[rnd], sub[rnd]
        yy = 2 * (cells >> 6) + (subs >> 1)
        xx = 2 * (cells & 63) + (subs & 1)
        pvec[rnd] = (yy * fine_w + xx)[0:1, :]
        req_out[rnd, 0:1, :] = yy[1:2, :]
        req_out[rnd, 1:2, :] = xx[1:2, :]
    p_cps = [
        pltpu.make_async_copy(pvec.at[0], psm0, lsem.at[1]),
        pltpu.make_async_copy(pvec.at[1], psm1, lsem.at[2]),
    ]
    for cp in p_cps:
        cp.start()
    map_cp.wait()

    @pl.loop(0, fine_h // 2)
    def _(i):
        rows = mapb[pl.ds(2 * i, 2)].reshape(2 * fine_w, width)
        mapf[pl.ds(pl.multiple_of(i * 2 * fine_w, 2 * fine_w), 2 * fine_w), :] = rows.astype(F32)

    for cp in p_cps:
        cp.wait()
    for rnd in range(2):

        @pl.loop(0, slots // 16)
        def _(g):
            for s in range(16):
                j = g * 16 + s
                qf[pl.ds(j, 1), :] = mapf[pl.ds((psm0, psm1)[rnd][0, j], 1), :]

        q_out[rnd] = qf[...].astype(BF16)

    @pl.when(home == 1)
    def _():
        tok_a.wait_send()

    @pl.when(home == 0)
    def _():
        tok_b.wait_send()

    q_cps = []
    for rnd in range(2):
        dev = opp_same if rnd == 0 else near_same
        for cp in (remote(req_out.at[rnd], req_in.at[rnd], 4 + rnd, dev), remote(q_out.at[rnd], q_in.at[rnd], 6 + rnd, dev)):
            cp.start()
            q_cps.append(cp)

    @pl.when(home == 1)
    def _():
        mat_b.wait_recv()
        tok_b.wait_recv()
        mat_f.start()
        tok_f.start()
        own_cp.wait()
        mleft[...] = mat[...]

    @pl.when(home == 0)
    def _():
        mat_a.wait_recv()
        tok_a.wait_recv()
        mat_f.wait_recv()
        tok_f.wait_recv()

    unit = scale * math.log2(math.e)
    block = 256

    def score_rows(i, m8):
        blk = pl.ds(pl.multiple_of(i * block, block), block)
        s = lax.dot_general(left[blk, :], right[...], (((1,), (1,)), ((), ())), preferred_element_type=F32) * unit
        scores[blk, :] = s
        m8 = jnp.maximum(m8, jnp.max(s.reshape(block // 8, 8, tok_count), axis=0))
        part = s[:, 0:128]
        for c in range(128, tok_count, 128):
            part = jnp.maximum(part, s[:, c : c + 128])
        top = jnp.max(part, axis=1, keepdims=True)
        tot = jnp.zeros((block, 128), F32)
        for c in range(0, tok_count, 128):
            tot = tot + jnp.exp2(scores[blk, c : c + 128] - top)
        lse = top * math.log(2.0) + jnp.log(jnp.sum(tot, axis=1, keepdims=True))
        hi = lse.astype(BF16).astype(F32)
        mid = (lse - hi).astype(BF16).astype(F32)
        lane = lax.broadcasted_iota(jnp.int32, (block, 128), 1)
        split = jnp.where(lane == 0, hi, jnp.where(lane == 1, mid, jnp.where(lane == 2, lse - hi - mid, 0.0)))
        lse_col[blk, :] = split.astype(BF16)
        return m8

    m8 = lax.fori_loop(0, tok_count // block, score_rows, jnp.full((8, tok_count), NEG, F32))
    top = jnp.max(m8, axis=0, keepdims=True)

    def score_cols(i, s8):
        s = scores[pl.ds(pl.multiple_of(i * 64, 64), 64), :]
        return s8 + jnp.sum(jnp.exp2(s - top).reshape(8, 8, tok_count), axis=0)

    s8 = lax.fori_loop(0, tok_count // 64, score_cols, jnp.zeros((8, tok_count), F32))
    lse = top * math.log(2.0) + jnp.log(jnp.sum(s8, axis=0, keepdims=True))
    hi = lse.astype(BF16).astype(F32)
    mid = (lse - hi).astype(BF16).astype(F32)
    pieces = jnp.concatenate([hi, mid, lse - hi - mid, jnp.zeros((13, tok_count), F32)], axis=0)
    pick = jnp.where(
        lax.broadcasted_iota(jnp.int32, (width, width), 0) == lax.broadcasted_iota(jnp.int32, (width, width), 1), 1.0, 0.0
    ).astype(BF16)
    flip = (((1,), (1,)), ((), ()))
    table_r[0:width, :] = lax.dot_general(pick, right[...], flip, preferred_element_type=F32).astype(BF16)
    table_r[width : width + 16, :] = pieces.astype(BF16)
    table_l[0:width, :] = lax.dot_general(pick, left[...], flip, preferred_element_type=F32).astype(BF16)
    table_l[width : width + 16, :] = lax.dot_general(
        pick[0:16, :], lse_col[...], flip, preferred_element_type=F32
    ).astype(BF16)

    ml, mr = mleft[1 * home], mright[1 * home]
    index[0:1, :] = jnp.concatenate([ml[0:1, :], mr[1:2, :]], axis=1)
    index[1:2, :] = jnp.concatenate([ml[1:2, :], mr[0:1, :]], axis=1)

    @pl.loop(0, 2 * slots // 256)
    def _(g):
        lane = pl.ds(pl.multiple_of(g * 256, 256), 256)
        got = []
        for side, table in enumerate((table_l, table_r)):
            want = index[side : side + 1, lane]
            tt = lax.broadcasted_iota(jnp.int32, (256, 256), 0).astype(F32).astype(BF16)
            hot = []
            for kb in range(tok_count // 256):
                w = jnp.broadcast_to((want - kb * 256).astype(F32), (16, 256)).astype(BF16)
                w = jnp.concatenate([w] * 16, axis=0)
                hot.append(jnp.where(tt == w, jnp.ones_like(w), jnp.zeros_like(w)))
            got.append(jnp.dot(table[...], jnp.concatenate(hot, axis=0), preferred_element_type=F32))
        gl, gr = got
        pair = jnp.sum(gl[0:width] * gr[0:width], axis=0, keepdims=True) * scale
        lses = jnp.sum(gl[width : width + 8] + gr[width : width + 8], axis=0, keepdims=True)
        conf_both[0:1, lane] = 2.0 * pair - lses + 2.0 * math.log(tok_count)

    conf = conf_both[...]
    conf_out[0] = conf[:, 0:slots]
    conf_out[1] = conf[:, slots:]
    conf_r = remote(conf_out.at[1], conf_in.at[home], 9 - home, at(near, home * core + (1 - home) * (1 - core)))
    conf_l = remote(conf_out.at[0], conf_in.at[0], 10, far_other)
    conf_w0 = remote(conf_out.at[1], conf_in.at[0], 9, near_other)
    conf_w1 = remote(conf_out.at[1], conf_in.at[1], 8, near_same)
    conf_r.start()

    @pl.when(home == 0)
    def _():
        conf_l.start()

    def refine(rnd):
        low8 = req_in[rnd, 0:1, :] - 2
        goal = []
        for r in range(5):
            t = r - low8 + 50
            goal.append(jnp.broadcast_to(low8 + t - 5 * ((t * 205) >> 10), (8, slots)))
        xmid = jnp.broadcast_to(req_in[rnd, 1:2, :], (8, slots))
        iota = lax.broadcasted_iota(jnp.int32, (8, slots), 0)
        unit = (width ** -0.5) * math.log2(math.e)

        def strip(xt, m8):
            strip_map = mapb[:, pl.ds(pl.multiple_of(xt * 16, 16), 16), :].reshape(fine_h * 16, width)
            parts = []
            for half in range(slots // 256):
                cols = slice(half * 256, half * 256 + 256)
                h = lax.dot_general(
                    strip_map, q_in[rnd, cols, :], (((1,), (1,)), ((), ())), preferred_element_type=F32
                )
                best = m8[:, cols]
                sums = [[None, None] for _ in range(5)]
                for r in range(5):
                    for k in range(2):
                        sums[r][k] = jnp.zeros((8, 256), F32)
                for yy in range(fine_h):
                    r = yy % 5
                    hit = goal[r][:, cols] == yy
                    for k in range(2):
                        sums[r][k] = jnp.where(hit, h[yy * 16 + k * 8 : yy * 16 + k * 8 + 8, :], sums[r][k])
                for k in range(2):
                    dx = iota[:, cols] + (xt * 16 + k * 8) - xmid[:, cols]
                    inside = jnp.abs(dx) <= 2
                    for r in range(5):
                        v = jnp.where(inside, sums[r][k] * unit, NEG)
                        best = jnp.maximum(best, v)
                        acc[r, pl.ds(pl.multiple_of(xt * 16 + k * 8, 8), 8), cols] = v
                parts.append(best)
            return jnp.concatenate(parts, axis=1)

        m8 = lax.fori_loop(0, fine_w // 16, strip, jnp.full((8, slots), NEG, F32))
        x1 = req_in[rnd, 1:2, :]
        missing = jnp.maximum(2 - x1, 0) + jnp.maximum(x1 - (fine_w - 3), 0)
        top = jnp.max(m8, axis=0, keepdims=True)
        top = jnp.where(missing > 0, jnp.maximum(top, 0.0), top)
        zero = jnp.where(missing > 0, jnp.exp2(-jnp.maximum(top, 0.0)), 0.0) * 5.0
        gone = jnp.where(x1 == 0, -3.0, 0.0) + jnp.where(x1 == 1, -2.0, 0.0)
        gone = gone + jnp.where(x1 == fine_w - 1, 3.0, 0.0) + jnp.where(x1 == fine_w - 2, 2.0, 0.0)
        for jt in range(slots // 128):
            lane = slice(jt * 128, jt * 128 + 128)
            topb = jnp.broadcast_to(top[:, lane], (8, 128))
            z = [jnp.zeros((8, 128), F32) for _ in range(5)]
            sx = jnp.zeros((8, 128), F32)
            dx = (iota[:, lane] - xmid[:, lane]).astype(F32)
            for xt in range(fine_w // 8):
                es = [jnp.exp2(acc[r, xt * 8 : xt * 8 + 8, lane] - topb) for r in range(5)]
                z = [a + e for a, e in zip(z, es)]
                sx = sx + (es[0] + es[1] + es[2] + es[3] + es[4]) * (dx + (8.0 * xt))
            sy = jnp.zeros((8, 128), F32)
            for r in range(5):
                sy = sy + z[r] * (goal[r][:, lane] - low8[:, lane] - 2).astype(F32)
            tot1 = jnp.sum(z[0] + z[1] + z[2] + z[3] + z[4], axis=0, keepdims=True)
            sx1 = jnp.sum(sx, axis=0, keepdims=True)
            sy1 = jnp.sum(sy, axis=0, keepdims=True)
            tot1 = tot1 + zero[:, lane] * missing[:, lane].astype(F32)
            sx1 = sx1 + zero[:, lane] * gone[:, lane]
            off_out[rnd, 0:1, lane] = sx1 / tot1
            off_out[rnd, 1:2, lane] = sy1 / tot1

    off_cps = []
    for rnd in range(2):
        q_cps[2 * rnd].wait_recv()
        q_cps[2 * rnd + 1].wait_recv()
        refine(rnd)
        cp = remote(off_out.at[rnd], off_in.at[rnd], 11 + rnd, opp_same if rnd == 0 else near_same)
        cp.start()
        off_cps.append(cp)

    for rnd in range(2):
        off_cps[rnd].wait_recv()
        res_ref[2 * rnd + 2 : 2 * rnd + 4, :] = off_in[rnd]

    @pl.when(home == 1)
    def _():
        conf_l.wait_recv()
        conf_in[1] = conf_out[0]

    @pl.when(home == 0)
    def _():
        conf_w0.wait_recv()
        conf_w1.wait_recv()

    for rnd in range(2):
        res_ref[rnd : rnd + 1, :] = conf_in[rnd]

    for cp in q_cps + off_cps + [conf_r]:
        cp.wait_send()

    @pl.when(home == 1)
    def _():
        mat_a.wait_send()
        mat_f.wait_send()
        tok_f.wait_send()

    @pl.when(home == 0)
    def _():
        mat_b.wait_send()
        conf_l.wait_send()


def finish(res_ref, cnt_ref, conf_ref, off_ref):
    for rnd in range(2):
        valid = lax.broadcasted_iota(jnp.int32, (2, res_ref.shape[1]), 1) < cnt_ref[0, rnd]
        conf_ref[0, rnd : rnd + 1, :] = jnp.where(valid[0:1, :], res_ref[rnd : rnd + 1, :], 0.0)
        off_ref[0, rnd] = jnp.where(valid, res_ref[2 * rnd + 2 : 2 * rnd + 4, :], 0.0)


def solution(mesh):
    devices = mesh.size

    def body(tokens, fine_map, matches, subcells, counts):
        tok_count, width = tokens.shape
        fine_h, fine_w, _ = fine_map.shape
        points = fine_h * fine_w
        slots = matches.shape[3]
        whole = pl.BlockSpec(memory_space=pltpu.VMEM)
        vmem = pltpu.VMEM
        raw = pl.pallas_call(
            lambda *refs: kernel(devices, *refs),
            name="match_refine",
            out_shape=jax.ShapeDtypeStruct((8, slots), F32),
            in_specs=[pl.BlockSpec(memory_space=pltpu.HBM)] * 4,
            out_specs=whole,
            scratch_shapes=[
                vmem((fine_h, fine_w, width), BF16),
                vmem((points, width), F32),
                vmem((tok_count, width), BF16),
                vmem((tok_count, width), BF16),
                vmem((2, 2, slots), jnp.int32),
                vmem((2, 2, slots), jnp.int32),
                vmem((2, 2, slots), jnp.int32),
                vmem((2, 2, slots), jnp.int32),
                vmem((2, 1, slots), jnp.int32),
                pltpu.SMEM((1, slots), jnp.int32),
                pltpu.SMEM((1, slots), jnp.int32),
                vmem((2, 2, slots), jnp.int32),
                vmem((2, 2, slots), jnp.int32),
                vmem((slots, width), F32),
                vmem((2, slots, width), BF16),
                vmem((2, slots, width), BF16),
                vmem((5, fine_w, slots), F32),
                vmem((tok_count, tok_count), F32),
                vmem((tok_count, 128), BF16),
                vmem((width + 16, tok_count), BF16),
                vmem((width + 16, tok_count), BF16),
                vmem((2, 2 * slots), jnp.int32),
                vmem((1, 2 * slots), F32),
                vmem((2, 2, slots), F32),
                vmem((2, 2, slots), F32),
                vmem((2, 1, slots), F32),
                vmem((2, 1, slots), F32),
                pltpu.SemaphoreType.DMA((4,)),
                pltpu.SemaphoreType.DMA((13,)),
                pltpu.SemaphoreType.DMA((13,)),
            ],
            compiler_params=pltpu.CompilerParams(
                collective_id=0, has_side_effects=True, vmem_limit_bytes=60 * 1024 * 1024
            ),
        )(tokens, fine_map, matches[0], subcells[0])
        return pl.pallas_call(
            finish,
            name="finish",
            out_shape=(
                jax.ShapeDtypeStruct((1, 2, slots), F32),
                jax.ShapeDtypeStruct((1, 2, 2, slots), F32),
            ),
            in_specs=[whole, pl.BlockSpec(memory_space=pltpu.SMEM)],
            out_specs=(whole, whole),
        )(raw, counts)

    return jax.shard_map(
        body,
        mesh=mesh,
        in_specs=(
            P("frame", None),
            P("frame", None, None),
            P("frame", None, None, None),
            P("frame", None, None, None),
            P("frame", None),
        ),
        out_specs=(P("frame", None, None), P("frame", None, None, None)),
        check_vma=False,
    )
```

```python
import math

import jax
import jax.numpy as jnp
from jax import lax
from jax.experimental import pallas as pl
from jax.experimental.pallas import tpu as pltpu
from jax.sharding import PartitionSpec as P

MESH = pl.DeviceIdType.MESH
F32 = jnp.float32
BF16 = jnp.bfloat16
NEG = -1e30
YRING = 8


def kernel(
    devices, tok_hbm, map_hbm, mat_hbm, sub_hbm, res_ref,
    mapb, mapf, left, right, mleft, mright, mat, sub, pvec, psm0, psm1, req_out, req_in, qf, q_out, q_in, q_two,
    acc, scores, lse_col, table_l, table_r, index, conf_both,
    off_out, off_in, conf_out, conf_in, lsem, ssem, rsem,
):
    tok_count, width = tok_hbm.shape
    fine_h, fine_w, _ = map_hbm.shape
    points = fine_h * fine_w
    slots = mat.shape[2]
    scale = 10.0 / width
    stride = devices // YRING
    me = lax.axis_index("frame")
    row = me // stride
    rest = me % stride
    core = rest % 2
    low = (row // 2) % 2
    home = (row // 4 + low + core + 1) % 2
    near = row + 2 - 4 * low
    opposite = (row + 4) % YRING
    far = (near + 4) % YRING

    def at(yy, cc):
        return (yy * stride + (rest - core) + cc,)

    sibling = at(row, 1 - core)
    near_same, near_other = at(near, core), at(near, 1 - core)
    opp_same, far_other = at(opposite, core), at(far, 1 - core)

    def remote(src, dst, i, dev):
        return pltpu.make_async_remote_copy(
            src_ref=src, dst_ref=dst, send_sem=ssem.at[i], recv_sem=rsem.at[i], device_id=dev, device_id_type=MESH
        )

    map_cp = pltpu.make_async_copy(map_hbm, mapb, lsem.at[0])
    mat_cp = pltpu.make_async_copy(mat_hbm, mat, lsem.at[1])
    sub_cp = pltpu.make_async_copy(sub_hbm, sub, lsem.at[2])
    own_cp = pltpu.make_async_copy(tok_hbm, left, lsem.at[3])
    mat_cp.start()
    sub_cp.start()
    map_cp.start()

    bar = pltpu.get_barrier_semaphore()
    peers = (sibling, near_same, near_other, opp_same, far_other)
    for peer in peers:
        pl.semaphore_signal(bar, inc=1, device_id=peer, device_id_type=MESH)
    pl.semaphore_wait(bar, len(peers))

    tok_a = remote(tok_hbm, left, 0, far_other)
    mat_a = remote(mat_hbm, mleft, 1, far_other)
    tok_b = remote(tok_hbm, right, 2, near_same)
    mat_b = remote(mat_hbm, mright, 3, near_same)
    tok_f = remote(right, right, 2, sibling)
    mat_f = remote(mright, mright, 3, sibling)

    @pl.when(home == 1)
    def _():
        mat_a.start()
        tok_a.start()
        own_cp.start()

    @pl.when(home == 0)
    def _():
        mat_b.start()
        tok_b.start()

    mat_cp.wait()
    sub_cp.wait()
    for rnd in range(2):
        cells, subs = mat[rnd], sub[rnd]
        yy = 2 * (cells >> 6) + (subs >> 1)
        xx = 2 * (cells & 63) + (subs & 1)
        pvec[rnd] = (yy * fine_w + xx)[0:1, :]
        req_out[rnd, 0:1, :] = yy[1:2, :]
        req_out[rnd, 1:2, :] = xx[1:2, :]
    p_cps = [
        pltpu.make_async_copy(pvec.at[0], psm0, lsem.at[1]),
        pltpu.make_async_copy(pvec.at[1], psm1, lsem.at[2]),
    ]
    for cp in p_cps:
        cp.start()
    map_cp.wait()

    @pl.loop(0, fine_h // 2)
    def _(i):
        rows = mapb[pl.ds(2 * i, 2)].reshape(2 * fine_w, width)
        mapf[pl.ds(pl.multiple_of(i * 2 * fine_w, 2 * fine_w), 2 * fine_w), :] = rows.astype(F32)

    for cp in p_cps:
        cp.wait()
    for rnd in range(2):

        @pl.loop(0, slots // 16)
        def _(g):
            for s in range(16):
                j = g * 16 + s
                qf[pl.ds(j, 1), :] = mapf[pl.ds((psm0, psm1)[rnd][0, j], 1), :]

        q_out[rnd] = qf[...].astype(BF16)

    q_cps = []
    for rnd in range(2):
        dev = opp_same if rnd == 0 else near_same
        q_cps.append(remote(req_out.at[rnd], req_in.at[rnd], 4 + rnd, dev))
        q_cps.append(remote(q_out.at[rnd], q_in.at[rnd], 6 + rnd, dev))

    @pl.when(home == 1)
    def _():
        mat_b.wait_recv()
        tok_b.wait_recv()
        mat_f.start()
        tok_f.start()
        q_cps[0].start()
        q_cps[1].start()
        q_cps[2].start()
        q_cps[3].start()
        own_cp.wait()
        mleft[...] = mat[...]

    @pl.when(home == 0)
    def _():
        mat_a.wait_recv()
        tok_a.wait_recv()
        q_cps[0].start()
        q_cps[1].start()
        q_cps[2].start()
        q_cps[3].start()
        mat_f.wait_recv()
        tok_f.wait_recv()

    unit = scale * math.log2(math.e)
    block = 256

    def score_rows(i, m8):
        blk = pl.ds(pl.multiple_of(i * block, block), block)
        s = lax.dot_general(left[blk, :], right[...], (((1,), (1,)), ((), ())), preferred_element_type=F32) * unit
        scores[blk, :] = s
        m8 = jnp.maximum(m8, jnp.max(s.reshape(block // 8, 8, tok_count), axis=0))
        part = s[:, 0:128]
        for c in range(128, tok_count, 128):
            part = jnp.maximum(part, s[:, c : c + 128])
        top = jnp.max(part, axis=1, keepdims=True)
        tot = jnp.zeros((block, 128), F32)
        for c in range(0, tok_count, 128):
            tot = tot + jnp.exp2(scores[blk, c : c + 128] - top)
        lse = top * math.log(2.0) + jnp.log(jnp.sum(tot, axis=1, keepdims=True))
        hi = lse.astype(BF16).astype(F32)
        mid = (lse - hi).astype(BF16).astype(F32)
        lane = lax.broadcasted_iota(jnp.int32, (block, 128), 1)
        split = jnp.where(lane == 0, hi, jnp.where(lane == 1, mid, jnp.where(lane == 2, lse - hi - mid, 0.0)))
        lse_col[blk, :] = split.astype(BF16)
        return m8

    m8 = lax.fori_loop(0, tok_count // block, score_rows, jnp.full((8, tok_count), NEG, F32))
    top = jnp.max(m8, axis=0, keepdims=True)

    def score_cols(i, s8):
        s = scores[pl.ds(pl.multiple_of(i * 64, 64), 64), :]
        return s8 + jnp.sum(jnp.exp2(s - top).reshape(8, 8, tok_count), axis=0)

    s8 = lax.fori_loop(0, tok_count // 64, score_cols, jnp.zeros((8, tok_count), F32))
    lse = top * math.log(2.0) + jnp.log(jnp.sum(s8, axis=0, keepdims=True))
    hi = lse.astype(BF16).astype(F32)
    mid = (lse - hi).astype(BF16).astype(F32)
    pieces = jnp.concatenate([hi, mid, lse - hi - mid, jnp.zeros((13, tok_count), F32)], axis=0)
    pick = jnp.where(
        lax.broadcasted_iota(jnp.int32, (width, width), 0) == lax.broadcasted_iota(jnp.int32, (width, width), 1), 1.0, 0.0
    ).astype(BF16)
    flip = (((1,), (1,)), ((), ()))
    table_r[0:width, :] = lax.dot_general(pick, right[...], flip, preferred_element_type=F32).astype(BF16)
    table_r[width : width + 16, :] = pieces.astype(BF16)
    table_l[0:width, :] = lax.dot_general(pick, left[...], flip, preferred_element_type=F32).astype(BF16)
    table_l[width : width + 16, :] = lax.dot_general(
        pick[0:16, :], lse_col[...], flip, preferred_element_type=F32
    ).astype(BF16)

    ml, mr = mleft[1 * home], mright[1 * home]
    index[0:1, :] = jnp.concatenate([ml[0:1, :], mr[1:2, :]], axis=1)
    index[1:2, :] = jnp.concatenate([ml[1:2, :], mr[0:1, :]], axis=1)

    @pl.loop(0, 2 * slots // 256)
    def _(g):
        lane = pl.ds(pl.multiple_of(g * 256, 256), 256)
        got = []
        for side, table in enumerate((table_l, table_r)):
            want = index[side : side + 1, lane]
            tt = lax.broadcasted_iota(jnp.int32, (256, 256), 0).astype(F32).astype(BF16)
            hot = []
            for kb in range(tok_count // 256):
                w = jnp.broadcast_to((want - kb * 256).astype(F32), (16, 256)).astype(BF16)
                w = jnp.concatenate([w] * 16, axis=0)
                hot.append(jnp.where(tt == w, jnp.ones_like(w), jnp.zeros_like(w)))
            got.append(jnp.dot(table[...], jnp.concatenate(hot, axis=0), preferred_element_type=F32))
        gl, gr = got
        pair = jnp.sum(gl[0:width] * gr[0:width], axis=0, keepdims=True) * scale
        lses = jnp.sum(gl[width : width + 8] + gr[width : width + 8], axis=0, keepdims=True)
        conf_both[0:1, lane] = 2.0 * pair - lses + 2.0 * math.log(tok_count)

    conf = conf_both[...]
    conf_out[0] = conf[:, 0:slots]
    conf_out[1] = conf[:, slots:]
    conf_r = remote(conf_out.at[1], conf_in.at[home], 9 - home, at(near, home * core + (1 - home) * (1 - core)))
    conf_l = remote(conf_out.at[0], conf_in.at[0], 10, far_other)
    conf_w0 = remote(conf_out.at[1], conf_in.at[0], 9, near_other)
    conf_w1 = remote(conf_out.at[1], conf_in.at[1], 8, near_same)
    conf_r.start()

    @pl.when(home == 0)
    def _():
        conf_l.start()

    def refine(rnd):
        upper = jnp.where(req_in[rnd, 0:1, :] >= fine_h // 2, 1, 0)
        flag = jnp.transpose(jnp.broadcast_to(upper.astype(F32), (width, slots)))
        q = q_in[rnd].astype(F32)
        q_two[:, 0:width] = jnp.where(flag > 0.5, 0.0, q).astype(BF16)
        q_two[:, width:] = jnp.where(flag > 0.5, q, 0.0).astype(BF16)
        shift = fine_h // 2 - 2
        tall = fine_h - shift
        low8 = req_in[rnd, 0:1, :] - 2 - shift * upper
        goal = []
        for r in range(5):
            t = r - low8 + 50
            goal.append(jnp.broadcast_to(low8 + t - 5 * ((t * 205) >> 10), (8, slots)))
        xmid = jnp.broadcast_to(req_in[rnd, 1:2, :], (8, slots))
        iota = lax.broadcasted_iota(jnp.int32, (8, slots), 0)
        unit = (width ** -0.5) * math.log2(math.e)

        def strip(xt, m8):
            cut = pl.ds(pl.multiple_of(xt * 16, 16), 16)
            strip_map = jnp.concatenate(
                [mapb[0:tall, cut, :].reshape(tall * 16, width), mapb[shift:, cut, :].reshape(tall * 16, width)], axis=1
            )
            parts = []
            for half in range(slots // 256):
                cols = slice(half * 256, half * 256 + 256)
                h = lax.dot_general(
                    strip_map, q_two[cols, :], (((1,), (1,)), ((), ())), preferred_element_type=F32
                )
                best = m8[:, cols]
                sums = [[None, None] for _ in range(5)]
                for r in range(5):
                    for k in range(2):
                        sums[r][k] = jnp.zeros((8, 256), F32)
                for yy in range(tall):
                    r = yy % 5
                    hit = goal[r][:, cols] == yy
                    for k in range(2):
                        sums[r][k] = jnp.where(hit, h[yy * 16 + k * 8 : yy * 16 + k * 8 + 8, :], sums[r][k])
                for k in range(2):
                    dx = iota[:, cols] + (xt * 16 + k * 8) - xmid[:, cols]
                    inside = jnp.abs(dx) <= 2
                    for r in range(5):
                        v = jnp.where(inside, sums[r][k] * unit, NEG)
                        best = jnp.maximum(best, v)
                        acc[r, pl.ds(pl.multiple_of(xt * 16 + k * 8, 8), 8), cols] = v
                parts.append(best)
            return jnp.concatenate(parts, axis=1)

        m8 = lax.fori_loop(0, fine_w // 16, strip, jnp.full((8, slots), NEG, F32))
        x1 = req_in[rnd, 1:2, :]
        missing = jnp.maximum(2 - x1, 0) + jnp.maximum(x1 - (fine_w - 3), 0)
        top = jnp.max(m8, axis=0, keepdims=True)
        top = jnp.where(missing > 0, jnp.maximum(top, 0.0), top)
        zero = jnp.where(missing > 0, jnp.exp2(-jnp.maximum(top, 0.0)), 0.0) * 5.0
        gone = jnp.where(x1 == 0, -3.0, 0.0) + jnp.where(x1 == 1, -2.0, 0.0)
        gone = gone + jnp.where(x1 == fine_w - 1, 3.0, 0.0) + jnp.where(x1 == fine_w - 2, 2.0, 0.0)
        for jt in range(slots // 128):
            lane = slice(jt * 128, jt * 128 + 128)
            topb = jnp.broadcast_to(top[:, lane], (8, 128))
            z = [jnp.zeros((8, 128), F32) for _ in range(5)]
            sx = jnp.zeros((8, 128), F32)
            dx = (iota[:, lane] - xmid[:, lane]).astype(F32)
            for xt in range(fine_w // 8):
                es = [jnp.exp2(acc[r, xt * 8 : xt * 8 + 8, lane] - topb) for r in range(5)]
                z = [a + e for a, e in zip(z, es)]
                sx = sx + (es[0] + es[1] + es[2] + es[3] + es[4]) * (dx + (8.0 * xt))
            sy = jnp.zeros((8, 128), F32)
            for r in range(5):
                sy = sy + z[r] * (goal[r][:, lane] - low8[:, lane] - 2).astype(F32)
            tot1 = jnp.sum(z[0] + z[1] + z[2] + z[3] + z[4], axis=0, keepdims=True)
            sx1 = jnp.sum(sx, axis=0, keepdims=True)
            sy1 = jnp.sum(sy, axis=0, keepdims=True)
            tot1 = tot1 + zero[:, lane] * missing[:, lane].astype(F32)
            sx1 = sx1 + zero[:, lane] * gone[:, lane]
            off_out[rnd, 0:1, lane] = sx1 / tot1
            off_out[rnd, 1:2, lane] = sy1 / tot1

    off_cps = []
    for rnd in range(2):
        q_cps[2 * rnd].wait_recv()
        q_cps[2 * rnd + 1].wait_recv()
        refine(rnd)
        cp = remote(off_out.at[rnd], off_in.at[rnd], 11 + rnd, opp_same if rnd == 0 else near_same)
        cp.start()
        off_cps.append(cp)

    for rnd in range(2):
        off_cps[rnd].wait_recv()
        res_ref[2 * rnd + 2 : 2 * rnd + 4, :] = off_in[rnd]

    @pl.when(home == 1)
    def _():
        conf_l.wait_recv()
        conf_in[1] = conf_out[0]

    @pl.when(home == 0)
    def _():
        conf_w0.wait_recv()
        conf_w1.wait_recv()

    for rnd in range(2):
        res_ref[rnd : rnd + 1, :] = conf_in[rnd]

    for cp in q_cps + off_cps + [conf_r]:
        cp.wait_send()

    @pl.when(home == 1)
    def _():
        mat_a.wait_send()
        tok_a.wait_send()
        mat_f.wait_send()
        tok_f.wait_send()

    @pl.when(home == 0)
    def _():
        mat_b.wait_send()
        tok_b.wait_send()
        conf_l.wait_send()


def finish(res_ref, cnt_ref, conf_ref, off_ref):
    for rnd in range(2):
        valid = lax.broadcasted_iota(jnp.int32, (2, res_ref.shape[1]), 1) < cnt_ref[0, rnd]
        conf_ref[0, rnd : rnd + 1, :] = jnp.where(valid[0:1, :], res_ref[rnd : rnd + 1, :], 0.0)
        off_ref[0, rnd] = jnp.where(valid, res_ref[2 * rnd + 2 : 2 * rnd + 4, :], 0.0)


def solution(mesh):
    devices = mesh.size

    def body(tokens, fine_map, matches, subcells, counts):
        tok_count, width = tokens.shape
        fine_h, fine_w, _ = fine_map.shape
        points = fine_h * fine_w
        slots = matches.shape[3]
        whole = pl.BlockSpec(memory_space=pltpu.VMEM)
        vmem = pltpu.VMEM
        raw = pl.pallas_call(
            lambda *refs: kernel(devices, *refs),
            name="match_refine",
            out_shape=jax.ShapeDtypeStruct((8, slots), F32),
            in_specs=[pl.BlockSpec(memory_space=pltpu.HBM)] * 4,
            out_specs=whole,
            scratch_shapes=[
                vmem((fine_h, fine_w, width), BF16),
                vmem((points, width), F32),
                vmem((tok_count, width), BF16),
                vmem((tok_count, width), BF16),
                vmem((2, 2, slots), jnp.int32),
                vmem((2, 2, slots), jnp.int32),
                vmem((2, 2, slots), jnp.int32),
                vmem((2, 2, slots), jnp.int32),
                vmem((2, 1, slots), jnp.int32),
                pltpu.SMEM((1, slots), jnp.int32),
                pltpu.SMEM((1, slots), jnp.int32),
                vmem((2, 2, slots), jnp.int32),
                vmem((2, 2, slots), jnp.int32),
                vmem((slots, width), F32),
                vmem((2, slots, width), BF16),
                vmem((2, slots, width), BF16),
                vmem((slots, 2 * width), BF16),
                vmem((5, fine_w, slots), F32),
                vmem((tok_count, tok_count), F32),
                vmem((tok_count, 128), BF16),
                vmem((width + 16, tok_count), BF16),
                vmem((width + 16, tok_count), BF16),
                vmem((2, 2 * slots), jnp.int32),
                vmem((1, 2 * slots), F32),
                vmem((2, 2, slots), F32),
                vmem((2, 2, slots), F32),
                vmem((2, 1, slots), F32),
                vmem((2, 1, slots), F32),
                pltpu.SemaphoreType.DMA((4,)),
                pltpu.SemaphoreType.DMA((13,)),
                pltpu.SemaphoreType.DMA((13,)),
            ],
            compiler_params=pltpu.CompilerParams(
                collective_id=0, has_side_effects=True, vmem_limit_bytes=60 * 1024 * 1024
            ),
        )(tokens, fine_map, matches[0], subcells[0])
        return pl.pallas_call(
            finish,
            name="finish",
            out_shape=(
                jax.ShapeDtypeStruct((1, 2, slots), F32),
                jax.ShapeDtypeStruct((1, 2, 2, slots), F32),
            ),
            in_specs=[whole, pl.BlockSpec(memory_space=pltpu.SMEM)],
            out_specs=(whole, whole),
        )(raw, counts)

    return jax.shard_map(
        body,
        mesh=mesh,
        in_specs=(
            P("frame", None),
            P("frame", None, None),
            P("frame", None, None, None),
            P("frame", None, None, None),
            P("frame", None),
        ),
        out_specs=(P("frame", None, None), P("frame", None, None, None)),
        check_vma=False,
    )
```

```python
import math

import jax
import jax.numpy as jnp
from jax import lax
from jax.experimental import pallas as pl
from jax.experimental.pallas import tpu as pltpu
from jax.sharding import PartitionSpec as P

MESH = pl.DeviceIdType.MESH
F32 = jnp.float32
BF16 = jnp.bfloat16
NEG = -1e30
YRING = 8


def kernel(
    devices, tok_hbm, map_hbm, mat_hbm, sub_hbm, res_ref,
    mapb, mapf, left, right, mleft, mright, mat, sub, pvec, psm0, psm1, req_out, req_in, qf, q_out, q_in, q_two,
    acc, scores, lse_col, table_l, table_r, index, conf_both,
    off_out, off_in, conf_out, conf_in, lsem, ssem, rsem,
):
    tok_count, width = tok_hbm.shape
    fine_h, fine_w, _ = map_hbm.shape
    points = fine_h * fine_w
    slots = mat.shape[2]
    scale = 10.0 / width
    stride = devices // YRING
    me = lax.axis_index("frame")
    row = me // stride
    rest = me % stride
    core = rest % 2
    low = (row // 2) % 2
    home = (row // 4 + low + core + 1) % 2
    near = row + 2 - 4 * low
    opposite = (row + 4) % YRING
    far = (near + 4) % YRING

    def at(yy, cc):
        return (yy * stride + (rest - core) + cc,)

    sibling = at(row, 1 - core)
    near_same, near_other = at(near, core), at(near, 1 - core)
    opp_same, far_other = at(opposite, core), at(far, 1 - core)

    def remote(src, dst, i, dev):
        return pltpu.make_async_remote_copy(
            src_ref=src, dst_ref=dst, send_sem=ssem.at[i], recv_sem=rsem.at[i], device_id=dev, device_id_type=MESH
        )

    map_cp = pltpu.make_async_copy(map_hbm, mapb, lsem.at[0])
    mat_cp = pltpu.make_async_copy(mat_hbm, mat, lsem.at[1])
    sub_cp = pltpu.make_async_copy(sub_hbm, sub, lsem.at[2])
    own_cp = pltpu.make_async_copy(tok_hbm, left, lsem.at[3])
    mat_cp.start()
    sub_cp.start()
    map_cp.start()

    bar = pltpu.get_barrier_semaphore()
    peers = (sibling, near_same, near_other, opp_same, far_other)
    for peer in peers:
        pl.semaphore_signal(bar, inc=1, device_id=peer, device_id_type=MESH)
    pl.semaphore_wait(bar, len(peers))

    tok_a = remote(tok_hbm, left, 0, far_other)
    mat_a = remote(mat_hbm, mleft, 1, far_other)
    tok_b = remote(tok_hbm, right, 2, near_same)
    mat_b = remote(mat_hbm, mright, 3, near_same)
    tok_f = remote(right, right, 2, sibling)
    mat_f = remote(mright, mright, 3, sibling)

    @pl.when(home == 1)
    def _():
        mat_a.start()
        tok_a.start()
        own_cp.start()

    @pl.when(home == 0)
    def _():
        mat_b.start()
        tok_b.start()

    mat_cp.wait()
    sub_cp.wait()
    for rnd in range(2):
        cells, subs = mat[rnd], sub[rnd]
        yy = 2 * (cells >> 6) + (subs >> 1)
        xx = 2 * (cells & 63) + (subs & 1)
        pvec[rnd] = (yy * fine_w + xx)[0:1, :]
        req_out[rnd, 0:1, :] = yy[1:2, :]
        req_out[rnd, 1:2, :] = xx[1:2, :]
    p_cps = [
        pltpu.make_async_copy(pvec.at[0], psm0, lsem.at[1]),
        pltpu.make_async_copy(pvec.at[1], psm1, lsem.at[2]),
    ]
    for cp in p_cps:
        cp.start()
    map_cp.wait()

    @pl.loop(0, fine_h // 2)
    def _(i):
        rows = mapb[pl.ds(2 * i, 2)].reshape(2 * fine_w, width)
        mapf[pl.ds(pl.multiple_of(i * 2 * fine_w, 2 * fine_w), 2 * fine_w), :] = rows.astype(F32)

    for cp in p_cps:
        cp.wait()
    for rnd in range(2):

        @pl.loop(0, slots // 16)
        def _(g):
            for s in range(16):
                j = g * 16 + s
                qf[pl.ds(j, 1), :] = mapf[pl.ds((psm0, psm1)[rnd][0, j], 1), :]

        q_out[rnd] = qf[...].astype(BF16)

    q_cps = []
    for rnd in range(2):
        dev = opp_same if rnd == 0 else near_same
        q_cps.append(remote(req_out.at[rnd], req_in.at[rnd], 4 + rnd, dev))
        q_cps.append(remote(q_out.at[rnd], q_in.at[rnd], 6 + rnd, dev))

    @pl.when(home == 1)
    def _():
        mat_b.wait_recv()
        tok_b.wait_recv()
        mat_f.start()
        tok_f.start()
        q_cps[0].start()
        q_cps[1].start()
        q_cps[2].start()
        q_cps[3].start()
        own_cp.wait()
        mleft[...] = mat[...]

    @pl.when(home == 0)
    def _():
        mat_a.wait_recv()
        tok_a.wait_recv()
        q_cps[0].start()
        q_cps[1].start()
        q_cps[2].start()
        q_cps[3].start()
        mat_f.wait_recv()
        tok_f.wait_recv()

    unit = scale * math.log2(math.e)
    block = 256

    def score_rows(i, m8):
        blk = pl.ds(pl.multiple_of(i * block, block), block)
        s = lax.dot_general(left[blk, :], right[...], (((1,), (1,)), ((), ())), preferred_element_type=F32) * unit
        scores[blk, :] = s
        m8 = jnp.maximum(m8, jnp.max(s.reshape(block // 8, 8, tok_count), axis=0))
        part = s[:, 0:128]
        for c in range(128, tok_count, 128):
            part = jnp.maximum(part, s[:, c : c + 128])
        top = jnp.max(part, axis=1, keepdims=True)
        tot = jnp.zeros((block, 128), F32)
        for c in range(0, tok_count, 128):
            tot = tot + jnp.exp2(scores[blk, c : c + 128] - top)
        lse = top * math.log(2.0) + jnp.log(jnp.sum(tot, axis=1, keepdims=True))
        hi = lse.astype(BF16).astype(F32)
        mid = (lse - hi).astype(BF16).astype(F32)
        lane = lax.broadcasted_iota(jnp.int32, (block, 128), 1)
        split = jnp.where(lane == 0, hi, jnp.where(lane == 1, mid, jnp.where(lane == 2, lse - hi - mid, 0.0)))
        lse_col[blk, :] = split.astype(BF16)
        return m8

    m8 = lax.fori_loop(0, tok_count // block, score_rows, jnp.full((8, tok_count), NEG, F32))
    top = jnp.max(m8, axis=0, keepdims=True)

    def score_cols(i, s8):
        s = scores[pl.ds(pl.multiple_of(i * 64, 64), 64), :]
        return s8 + jnp.sum(jnp.exp2(s - top).reshape(8, 8, tok_count), axis=0)

    s8 = lax.fori_loop(0, tok_count // 64, score_cols, jnp.zeros((8, tok_count), F32))
    lse = top * math.log(2.0) + jnp.log(jnp.sum(s8, axis=0, keepdims=True))
    hi = lse.astype(BF16).astype(F32)
    mid = (lse - hi).astype(BF16).astype(F32)
    pieces = jnp.concatenate([hi, mid, lse - hi - mid, jnp.zeros((13, tok_count), F32)], axis=0)
    pick = jnp.where(
        lax.broadcasted_iota(jnp.int32, (width, width), 0) == lax.broadcasted_iota(jnp.int32, (width, width), 1), 1.0, 0.0
    ).astype(BF16)
    flip = (((1,), (1,)), ((), ()))
    table_r[0:width, :] = lax.dot_general(pick, right[...], flip, preferred_element_type=F32).astype(BF16)
    table_r[width : width + 16, :] = pieces.astype(BF16)
    table_l[0:width, :] = lax.dot_general(pick, left[...], flip, preferred_element_type=F32).astype(BF16)
    table_l[width : width + 16, :] = lax.dot_general(
        pick[0:16, :], lse_col[...], flip, preferred_element_type=F32
    ).astype(BF16)

    ml, mr = mleft[1 * home], mright[1 * home]
    index[0:1, :] = jnp.concatenate([ml[0:1, :], mr[1:2, :]], axis=1)
    index[1:2, :] = jnp.concatenate([ml[1:2, :], mr[0:1, :]], axis=1)

    @pl.loop(0, 2 * slots // 256)
    def _(g):
        lane = pl.ds(pl.multiple_of(g * 256, 256), 256)
        got = []
        for side, table in enumerate((table_l, table_r)):
            want = index[side : side + 1, lane]
            tt = lax.broadcasted_iota(jnp.int32, (256, 256), 0).astype(F32).astype(BF16)
            hot = []
            for kb in range(tok_count // 256):
                w = jnp.broadcast_to((want - kb * 256).astype(F32), (16, 256)).astype(BF16)
                w = jnp.concatenate([w] * 16, axis=0)
                hot.append(jnp.where(tt == w, jnp.ones_like(w), jnp.zeros_like(w)))
            got.append(jnp.dot(table[...], jnp.concatenate(hot, axis=0), preferred_element_type=F32))
        gl, gr = got
        pair = jnp.sum(gl[0:width] * gr[0:width], axis=0, keepdims=True) * scale
        lses = jnp.sum(gl[width : width + 8] + gr[width : width + 8], axis=0, keepdims=True)
        conf_both[0:1, lane] = 2.0 * pair - lses + 2.0 * math.log(tok_count)

    conf = conf_both[...]
    conf_out[0] = conf[:, 0:slots]
    conf_out[1] = conf[:, slots:]
    conf_r = remote(conf_out.at[1], conf_in.at[home], 9 - home, at(near, home * core + (1 - home) * (1 - core)))
    conf_l = remote(conf_out.at[0], conf_in.at[0], 10, far_other)
    conf_w0 = remote(conf_out.at[1], conf_in.at[0], 9, near_other)
    conf_w1 = remote(conf_out.at[1], conf_in.at[1], 8, near_same)
    conf_r.start()

    @pl.when(home == 0)
    def _():
        conf_l.start()

    def refine(rnd):
        upper = jnp.where(req_in[rnd, 0:1, :] >= fine_h // 2, 1, 0)
        flag = jnp.transpose(jnp.broadcast_to(upper.astype(F32), (width, slots)))
        q = q_in[rnd].astype(F32)
        q_two[:, 0:width] = jnp.where(flag > 0.5, 0.0, q).astype(BF16)
        q_two[:, width:] = jnp.where(flag > 0.5, q, 0.0).astype(BF16)
        shift = fine_h // 2 - 2
        tall = fine_h - shift
        low8 = req_in[rnd, 0:1, :] - 2 - shift * upper
        goal = []
        for r in range(5):
            t = r - low8 + 50
            goal.append(jnp.broadcast_to(low8 + t - 5 * ((t * 205) >> 10), (8, slots)))
        xmid = jnp.broadcast_to(req_in[rnd, 1:2, :], (8, slots))
        iota = lax.broadcasted_iota(jnp.int32, (8, slots), 0)
        unit = (width ** -0.5) * math.log2(math.e)

        def strip(xt, m8):
            cut = pl.ds(pl.multiple_of(xt * 16, 16), 16)
            strip_map = jnp.concatenate(
                [mapb[0:tall, cut, :].reshape(tall * 16, width), mapb[shift:, cut, :].reshape(tall * 16, width)], axis=1
            )
            parts = []
            for half in range(slots // 256):
                cols = slice(half * 256, half * 256 + 256)
                h = lax.dot_general(
                    strip_map, q_two[cols, :], (((1,), (1,)), ((), ())), preferred_element_type=F32
                )
                best = m8[:, cols]
                sums = [[None, None] for _ in range(5)]
                for r in range(5):
                    for k in range(2):
                        sums[r][k] = jnp.zeros((8, 256), F32)
                for yy in range(tall):
                    r = yy % 5
                    hit = goal[r][:, cols] == yy
                    for k in range(2):
                        sums[r][k] = jnp.where(hit, h[yy * 16 + k * 8 : yy * 16 + k * 8 + 8, :], sums[r][k])
                for k in range(2):
                    dx = iota[:, cols] + (xt * 16 + k * 8) - xmid[:, cols]
                    inside = jnp.abs(dx) <= 2
                    for r in range(5):
                        v = jnp.where(inside, sums[r][k] * unit, NEG)
                        best = jnp.maximum(best, v)
                        acc[r, pl.ds(pl.multiple_of(xt * 16 + k * 8, 8), 8), cols] = v
                parts.append(best)
            return jnp.concatenate(parts, axis=1)

        m8 = lax.fori_loop(0, fine_w // 16, strip, jnp.full((8, slots), NEG, F32), unroll=2)
        x1 = req_in[rnd, 1:2, :]
        missing = jnp.maximum(2 - x1, 0) + jnp.maximum(x1 - (fine_w - 3), 0)
        top = jnp.max(m8, axis=0, keepdims=True)
        top = jnp.where(missing > 0, jnp.maximum(top, 0.0), top)
        zero = jnp.where(missing > 0, jnp.exp2(-jnp.maximum(top, 0.0)), 0.0) * 5.0
        gone = jnp.where(x1 == 0, -3.0, 0.0) + jnp.where(x1 == 1, -2.0, 0.0)
        gone = gone + jnp.where(x1 == fine_w - 1, 3.0, 0.0) + jnp.where(x1 == fine_w - 2, 2.0, 0.0)
        for jt in range(slots // 128):
            lane = slice(jt * 128, jt * 128 + 128)
            topb = jnp.broadcast_to(top[:, lane], (8, 128))
            z = [jnp.zeros((8, 128), F32) for _ in range(5)]
            sx = jnp.zeros((8, 128), F32)
            dx = (iota[:, lane] - xmid[:, lane]).astype(F32)
            for xt in range(fine_w // 8):
                es = [jnp.exp2(acc[r, xt * 8 : xt * 8 + 8, lane] - topb) for r in range(5)]
                z = [a + e for a, e in zip(z, es)]
                sx = sx + (es[0] + es[1] + es[2] + es[3] + es[4]) * (dx + (8.0 * xt))
            sy = jnp.zeros((8, 128), F32)
            for r in range(5):
                sy = sy + z[r] * (goal[r][:, lane] - low8[:, lane] - 2).astype(F32)
            tot1 = jnp.sum(z[0] + z[1] + z[2] + z[3] + z[4], axis=0, keepdims=True)
            sx1 = jnp.sum(sx, axis=0, keepdims=True)
            sy1 = jnp.sum(sy, axis=0, keepdims=True)
            tot1 = tot1 + zero[:, lane] * missing[:, lane].astype(F32)
            sx1 = sx1 + zero[:, lane] * gone[:, lane]
            off_out[rnd, 0:1, lane] = sx1 / tot1
            off_out[rnd, 1:2, lane] = sy1 / tot1

    off_cps = []
    for rnd in range(2):
        q_cps[2 * rnd].wait_recv()
        q_cps[2 * rnd + 1].wait_recv()
        refine(rnd)
        cp = remote(off_out.at[rnd], off_in.at[rnd], 11 + rnd, opp_same if rnd == 0 else near_same)
        cp.start()
        off_cps.append(cp)

    for rnd in range(2):
        off_cps[rnd].wait_recv()
        res_ref[2 * rnd + 2 : 2 * rnd + 4, :] = off_in[rnd]

    @pl.when(home == 1)
    def _():
        conf_l.wait_recv()
        conf_in[1] = conf_out[0]

    @pl.when(home == 0)
    def _():
        conf_w0.wait_recv()
        conf_w1.wait_recv()

    for rnd in range(2):
        res_ref[rnd : rnd + 1, :] = conf_in[rnd]

    for cp in q_cps + off_cps + [conf_r]:
        cp.wait_send()

    @pl.when(home == 1)
    def _():
        mat_a.wait_send()
        tok_a.wait_send()
        mat_f.wait_send()
        tok_f.wait_send()

    @pl.when(home == 0)
    def _():
        mat_b.wait_send()
        tok_b.wait_send()
        conf_l.wait_send()


def finish(res_ref, cnt_ref, conf_ref, off_ref):
    for rnd in range(2):
        valid = lax.broadcasted_iota(jnp.int32, (2, res_ref.shape[1]), 1) < cnt_ref[0, rnd]
        conf_ref[0, rnd : rnd + 1, :] = jnp.where(valid[0:1, :], res_ref[rnd : rnd + 1, :], 0.0)
        off_ref[0, rnd] = jnp.where(valid, res_ref[2 * rnd + 2 : 2 * rnd + 4, :], 0.0)


def solution(mesh):
    devices = mesh.size

    def body(tokens, fine_map, matches, subcells, counts):
        tok_count, width = tokens.shape
        fine_h, fine_w, _ = fine_map.shape
        points = fine_h * fine_w
        slots = matches.shape[3]
        whole = pl.BlockSpec(memory_space=pltpu.VMEM)
        vmem = pltpu.VMEM
        raw = pl.pallas_call(
            lambda *refs: kernel(devices, *refs),
            name="match_refine",
            out_shape=jax.ShapeDtypeStruct((8, slots), F32),
            in_specs=[pl.BlockSpec(memory_space=pltpu.HBM)] * 4,
            out_specs=whole,
            scratch_shapes=[
                vmem((fine_h, fine_w, width), BF16),
                vmem((points, width), F32),
                vmem((tok_count, width), BF16),
                vmem((tok_count, width), BF16),
                vmem((2, 2, slots), jnp.int32),
                vmem((2, 2, slots), jnp.int32),
                vmem((2, 2, slots), jnp.int32),
                vmem((2, 2, slots), jnp.int32),
                vmem((2, 1, slots), jnp.int32),
                pltpu.SMEM((1, slots), jnp.int32),
                pltpu.SMEM((1, slots), jnp.int32),
                vmem((2, 2, slots), jnp.int32),
                vmem((2, 2, slots), jnp.int32),
                vmem((slots, width), F32),
                vmem((2, slots, width), BF16),
                vmem((2, slots, width), BF16),
                vmem((slots, 2 * width), BF16),
                vmem((5, fine_w, slots), F32),
                vmem((tok_count, tok_count), F32),
                vmem((tok_count, 128), BF16),
                vmem((width + 16, tok_count), BF16),
                vmem((width + 16, tok_count), BF16),
                vmem((2, 2 * slots), jnp.int32),
                vmem((1, 2 * slots), F32),
                vmem((2, 2, slots), F32),
                vmem((2, 2, slots), F32),
                vmem((2, 1, slots), F32),
                vmem((2, 1, slots), F32),
                pltpu.SemaphoreType.DMA((4,)),
                pltpu.SemaphoreType.DMA((13,)),
                pltpu.SemaphoreType.DMA((13,)),
            ],
            compiler_params=pltpu.CompilerParams(
                collective_id=0, has_side_effects=True, vmem_limit_bytes=60 * 1024 * 1024
            ),
        )(tokens, fine_map, matches[0], subcells[0])
        return pl.pallas_call(
            finish,
            name="finish",
            out_shape=(
                jax.ShapeDtypeStruct((1, 2, slots), F32),
                jax.ShapeDtypeStruct((1, 2, 2, slots), F32),
            ),
            in_specs=[whole, pl.BlockSpec(memory_space=pltpu.SMEM)],
            out_specs=(whole, whole),
        )(raw, counts)

    return jax.shard_map(
        body,
        mesh=mesh,
        in_specs=(
            P("frame", None),
            P("frame", None, None),
            P("frame", None, None, None),
            P("frame", None, None, None),
            P("frame", None),
        ),
        out_specs=(P("frame", None, None), P("frame", None, None, None)),
        check_vma=False,
    )
```
